256 devices in a mesh: member: 16 (over x, y_lo, core), sub: 16 (over y_hi, z).
Axes of the slice: x: 4, y: 4 (y_hi: 2, y_lo: 2; y = y_hi * 2 + y_lo), z: 8, core: 2. Of those that a mesh axis runs over, the one named last changes fastest.
Arguments:
- velocity: float32 [16, 3, 256, 32, 128], P('member', None, 'sub'), may hold values from -8 to 8
- forcing: float32 [16, 3, 256, 32, 128], P('member', None, 'sub'), may hold values from -16 to 16
Outputs:
- new_velocity: float32 [16, 3, 256, 32, 128], P('member', None, 'sub')
The draws below stay inside these ranges and needn't reach their ends.
All inputs are finite; a program needn't handle non-finite values.
Results may differ from the reference program's by a relative error of at most 0.00029.
Values sent between devices are 32-bit elements; how exact they have to be, the bound alone decides.
A program may use at most 64 MiB of HBM per device.

```python
import math
import jax
import jax.numpy as jnp
from jax import lax

NY = 32
NZ = 128
SWEEPS = 8
MEMBERS = 16
NX = 256


def draw_velocity(key, part):
    layer_key, noise_key = jax.random.split(key, 2)
    full_shape = (MEMBERS, 3, NX, NY, NZ)
    layer_scale = jnp.exp(jax.random.uniform(layer_key, (NX,), jnp.float32, math.log(1.5), math.log(5.0)))
    noise_draw = jax.random.normal(noise_key, full_shape, jnp.float32)
    values = noise_draw * layer_scale[None, None, :, None, None]
    return jnp.clip(values, -8.0, 8.0)


def draw_forcing(key, part):
    rough_key, amp_key, phase_key, sign_key = jax.random.split(key, 4)
    full_shape = (MEMBERS, 3, NX, NY, NZ)
    rough_part = jnp.clip(2.0 * jax.random.normal(rough_key, full_shape, jnp.float32), -8.0, 8.0)
    amplitude = jnp.exp(jax.random.uniform(amp_key, (MEMBERS, 3), jnp.float32, math.log(2.0), math.log(4.0)))
    phases = jax.random.uniform(phase_key, (MEMBERS, 3, 2), jnp.float32, -math.pi, math.pi)
    signs = jnp.where(jax.random.bernoulli(sign_key, 0.5, (MEMBERS, 3)), 1.0, -1.0).astype(jnp.float32)
    along_x = 2.0 * math.pi * jnp.arange(NX).astype(jnp.float32) / NX
    along_y = 2.0 * math.pi * jnp.arange(NY).astype(jnp.float32) / NY
    profile_x = 1.0 + 0.6 * jnp.cos(along_x[None, None, :] + phases[:, :, 0:1])
    profile_y = 1.0 + 0.25 * jnp.cos(along_y[None, None, :] + phases[:, :, 1:2])
    smooth_part = (signs * amplitude)[:, :, None, None, None] * profile_x[:, :, :, None, None] * profile_y[:, :, None, :, None]
    return jnp.clip(rough_part + smooth_part, -16.0, 16.0)


def setup_inputs(seed: int = 0) -> dict:
    seeds = jax.random.split(jax.random.key(seed), 3)
    velocity = draw_velocity(jax.random.fold_in(seeds[2], 71), 0)
    forcing = draw_forcing(jax.random.fold_in(seeds[2], 71), 0)
    return dict(velocity=velocity, forcing=forcing)


TIME_STEP = 0.25
EDDY_COEFF = 1.0
BASE_VISCOSITY = 1.0
LOWER_EDGE = 0.1
UPPER_EDGE = 1.9


def step_sizes(sweep_count):
    middle = (UPPER_EDGE + LOWER_EDGE) / 2
    radius = (UPPER_EDGE - LOWER_EDGE) / 2
    return [1.0 / (middle + radius * math.cos(math.pi * (2 * position + 1) / (2 * sweep_count))) for position in range(sweep_count)]


def reference(velocity, forcing):
    members = velocity.shape[0]
    mean_flow = jnp.sum(velocity, 0) / members
    spread = jnp.sum(jnp.sum((velocity - mean_flow) ** 2, 1), 0) / members
    viscosity = BASE_VISCOSITY + EDDY_COEFF * TIME_STEP * spread
    faces = []
    for grid_axis in range(3):
        faces.append(0.5 * (viscosity + jnp.roll(viscosity, -1, grid_axis)))
        faces.append(0.5 * (viscosity + jnp.roll(viscosity, 1, grid_axis)))
    diagonal = 1.0 + TIME_STEP * (faces[0] + faces[1] + faces[2] + faces[3] + faces[4] + faces[5])
    sizes_list = step_sizes(SWEEPS)

    def operator(field):
        neighbours = faces[0] * jnp.roll(field, -1, 1) + faces[1] * jnp.roll(field, 1, 1)
        neighbours = neighbours + faces[2] * jnp.roll(field, -1, 2) + faces[3] * jnp.roll(field, 1, 2)
        neighbours = neighbours + faces[4] * jnp.roll(field, -1, 3) + faces[5] * jnp.roll(field, 1, 3)
        return diagonal * field - TIME_STEP * neighbours

    def advance(member_pair):
        member_velocity, member_forcing = member_pair
        terms = [mean_flow[grid_axis] * ((jnp.roll(member_velocity, -1, grid_axis + 1) - jnp.roll(member_velocity, 1, grid_axis + 1)) * 0.5) for grid_axis in range(3)]
        transport = terms[0] + terms[1] + terms[2]
        source = member_velocity - TIME_STEP * transport + TIME_STEP * member_forcing
        field = source
        for step_size in sizes_list:
            field = field + step_size * (source - operator(field)) / diagonal
        return field

    return lax.map(advance, (velocity, forcing))
```

```python
import functools
import math

import jax
import jax.numpy as jnp
from jax import lax
from jax.experimental import pallas as pl
from jax.experimental.pallas import tpu as pltpu
from jax.sharding import PartitionSpec as P

MESH = pl.DeviceIdType.MESH
SWEEPS = 8
TIME_STEP = 0.25
EDDY_COEFF = 1.0
BASE_VISCOSITY = 1.0
LOWER_EDGE = 0.1
UPPER_EDGE = 1.9

LAYERS = 16
TILES = 4
ROWS = 8
LANES = 128
CHIPS = 8
HALO = 4
ORDER = ((2, 1), (1, 1), (3, 1), (2, 0), (1, 0), (3, 0), (0, 1))


def step_sizes(sweep_count):
    middle = (UPPER_EDGE + LOWER_EDGE) / 2
    radius = (UPPER_EDGE - LOWER_EDGE) / 2
    return [
        1.0 / (middle + radius * math.cos(math.pi * (2 * position + 1) / (2 * sweep_count)))
        for position in range(sweep_count)
    ]


def shifted_chip(chip, dx, dy):
    x, y = chip // 2, lax.rem(chip, 2)
    return lax.rem(x + dx, 4) * 2 + lax.rem(y + dy, 2)


def kernel(
    vel_ref, force_ref, out_ref,
    vel, force, partner_vel, sums, arrived, flow, nu, weights, source, field_a, field_b, field_c, halo_low, halo_high,
    load_sem, pair_sem, rs_send, rs_recv, ag_send, ag_recv, fw_send, fw_recv,
    vh_send, vh_recv, nu_send, nu_recv, src_send, src_recv, mid_send, mid_recv,
):
    member, sub = lax.axis_index("member"), lax.axis_index("sub")
    chip, core = member // 2, lax.rem(member, 2)
    subs = lax.axis_size("sub")
    above = (member, lax.rem(sub + 1, subs))
    below = (member, lax.rem(sub + subs - 1, subs))
    partner = (chip * 2 + 1 - core, sub)
    peers = [(shifted_chip(chip, dx, dy) * 2 + core, sub) for dx, dy in ORDER]
    targets = [shifted_chip(chip, dx, dy) for dx, dy in ORDER]
    origins = [shifted_chip(chip, 4 - dx, dy) for dx, dy in ORDER]

    def remote(src, dst, send, recv, device):
        return pltpu.make_async_remote_copy(
            src_ref=src, dst_ref=dst, send_sem=send, recv_sem=recv, device_id=device, device_id_type=MESH
        )

    load_vel = pltpu.make_async_copy(vel_ref, vel.at[:, pl.ds(1, LAYERS)], load_sem.at[0])
    load_force = pltpu.make_async_copy(force_ref, force, load_sem.at[1])
    load_vel.start()
    load_force.start()

    barrier = pltpu.get_barrier_semaphore()
    greeted = [*peers, partner, above, below]
    for device in greeted:
        pl.semaphore_signal(barrier, inc=1, device_id=device, device_id_type=MESH)
    pl.semaphore_wait(barrier, len(greeted))

    pair = remote(
        vel_ref.at[:, pl.ds((1 - core) * CHIPS, CHIPS)], partner_vel, pair_sem.at[0], pair_sem.at[1], partner
    )
    pair.start()
    load_vel.wait()
    pair.wait_recv()

    rs_copies = []
    for tile in range(TILES):
        rows = pl.ds(tile, ROWS, stride=TILES)

        def pair_sums(target, tile=tile, rows=rows):
            squares = None
            for axis in range(3):
                mine = vel[axis, 1 + core * CHIPS + target, rows, :]
                other = partner_vel[axis, target, rows, :]
                sums[tile, target, axis] = mine + other
                term = mine * mine + other * other
                squares = term if squares is None else squares + term
            sums[tile, target, 3] = squares

        for target in targets:
            pair_sums(target)
        pair_sums(chip)
        for place, target in enumerate(targets):
            copy = remote(
                sums.at[tile, target], arrived.at[tile, chip], rs_send.at[tile, place], rs_recv.at[tile, chip],
                peers[place],
            )
            copy.start()
            rs_copies.append(copy)

    vel_up = remote(vel_ref.at[:, LAYERS - 1], vel.at[:, 0], vh_send.at[0], vh_recv.at[0], above)
    vel_down = remote(vel_ref.at[:, 0], vel.at[:, LAYERS + 1], vh_send.at[1], vh_recv.at[1], below)
    vel_up.start()
    vel_down.start()

    own = core * CHIPS + chip
    ag_copies = []
    for tile in range(TILES):
        for origin in origins:
            remote(
                sums.at[tile, 0], arrived.at[tile, origin], rs_send.at[tile, 0], rs_recv.at[tile, origin], partner
            ).wait_recv()
        total = [
            (
                (sums[tile, chip, i] + arrived[tile, origins[0], i])
                + (arrived[tile, origins[1], i] + arrived[tile, origins[2], i])
            )
            + (
                (arrived[tile, origins[3], i] + arrived[tile, origins[4], i])
                + (arrived[tile, origins[5], i] + arrived[tile, origins[6], i])
            )
            for i in range(4)
        ]
        mean = [total[i] * (1.0 / 16) for i in range(3)]
        spread = total[3] * (1.0 / 16) - (mean[0] * mean[0] + mean[1] * mean[1] + mean[2] * mean[2])
        for i in range(3):
            flow[own, tile, i] = mean[i]
        flow[own, tile, 3] = BASE_VISCOSITY + EDDY_COEFF * TIME_STEP * spread
        for place in range(len(ORDER)):
            copy = remote(
                flow.at[own, tile], flow.at[own, tile], ag_send.at[tile, place], ag_recv.at[tile, chip], peers[place]
            )
            copy.start()
            ag_copies.append(copy)

    load_force.wait()
    vel_up.wait_recv()
    vel_down.wait_recv()

    def make_source(layer):
        for axis in range(3):
            tiles = [vel[axis, layer + 1, pl.ds(t, ROWS, stride=TILES), :] for t in range(TILES)]
            for t in range(TILES):
                rows = pl.ds(t, ROWS, stride=TILES)
                here = tiles[t]
                along_x = vel[axis, layer + 2, rows, :] - vel[axis, layer, rows, :]
                north = tiles[t + 1] if t + 1 < TILES else pltpu.roll(tiles[0], ROWS - 1, 0)
                south = tiles[t - 1] if t > 0 else pltpu.roll(tiles[TILES - 1], 1, 0)
                along_z = pltpu.roll(here, LANES - 1, 1) - pltpu.roll(here, 1, 1)
                moved = flow[layer, t, 0] * along_x + flow[layer, t, 1] * (north - south) + flow[layer, t, 2] * along_z
                field_a[axis, HALO + layer, t] = (
                    here + TIME_STEP * force[axis, layer, rows, :] - (0.5 * TIME_STEP) * moved
                )
        for t in range(TILES):
            nu[HALO + layer, t] = flow[layer, t, 3]

    def chip_at(k):
        return shifted_chip(chip, k // 2, lax.rem(k, 2))

    def forward(at):
        layer = core * CHIPS + at
        return remote(flow.at[layer], flow.at[layer], fw_send.at[at], fw_recv.at[at], partner)

    def gather_step(k, carry):
        @pl.when(k < CHIPS)
        def _():
            at = chip_at(k)
            layer = core * CHIPS + at

            @pl.when(k > 0)
            def _():
                for tile in range(TILES):
                    remote(
                        flow.at[layer, tile], flow.at[layer, tile], ag_send.at[tile, 0], ag_recv.at[tile, at], partner
                    ).wait_recv()

            forward(at).start()
            make_source(layer)

        @pl.when(k > 0)
        def _():
            at = chip_at(k - 1)
            layer = (1 - core) * CHIPS + at
            remote(flow.at[layer], flow.at[layer], fw_send.at[at], fw_recv.at[at], partner).wait_recv()
            make_source(layer)

        return carry

    lax.fori_loop(0, CHIPS + 1, gather_step, 0)

    low, high = pl.ds(HALO, HALO), pl.ds(LAYERS, HALO)
    before, after = pl.ds(0, HALO), pl.ds(HALO + LAYERS, HALO)
    nu_copies = [
        remote(nu.at[low], nu.at[after], nu_send.at[0], nu_recv.at[0], below),
        remote(nu.at[high], nu.at[before], nu_send.at[1], nu_recv.at[1], above),
    ]
    for copy in nu_copies:
        copy.start()

    def source_copies(axis):
        return [
            remote(
                field_a.at[axis, low], field_a.at[axis, after], src_send.at[0, axis], src_recv.at[0, axis], below
            ),
            remote(
                field_a.at[axis, high], field_a.at[axis, before], src_send.at[1, axis], src_recv.at[1, axis], above
            ),
        ]

    for axis in range(3):
        for copy in source_copies(axis):
            copy.start()

    def make_weights(layer):
        centre = [nu[layer, t] for t in range(TILES)]
        for t in range(TILES):
            here = centre[t]
            north = centre[t + 1] if t + 1 < TILES else pltpu.roll(centre[0], ROWS - 1, 0)
            south = centre[t - 1] if t > 0 else pltpu.roll(centre[TILES - 1], 1, 0)
            around = (
                nu[layer + 1, t], nu[layer - 1, t], north, south,
                pltpu.roll(here, LANES - 1, 1), pltpu.roll(here, 1, 1),
            )
            faces = [here + other for other in around]
            total = ((faces[0] + faces[1]) + (faces[2] + faces[3])) + (faces[4] + faces[5])
            inverse = 1.0 / (1.0 + (0.5 * TIME_STEP) * total)
            scaled = (0.5 * TIME_STEP) * inverse
            for i in range(6):
                weights[layer, i, t] = faces[i] * scaled
            weights[layer, 6, t] = inverse

    def scale_source(layer, axis):
        for t in range(TILES):
            source[axis, layer, t] = field_a[axis, layer, t] * weights[layer, 6, t]

    def inner_weights(layer, carry):
        make_weights(layer)
        for axis in range(3):
            scale_source(layer, axis)
        return carry

    lax.fori_loop(HALO + 1, HALO + LAYERS - 1, inner_weights, 0)

    sizes = step_sizes(SWEEPS)

    def field_at(level):
        if level % HALO == 0:
            return field_a
        return (field_c, field_b)[level % 2]

    def sweep_tile(level, layer, axis, t, tiles, factors):
        old, new = field_at(level - 1), field_at(level)
        here = tiles[t]
        north = tiles[t + 1] if t + 1 < TILES else pltpu.roll(tiles[0], ROWS - 1, 0)
        south = tiles[t - 1] if t > 0 else pltpu.roll(tiles[TILES - 1], 1, 0)
        part_x = factors[0] * old[axis, layer + 1, t] + factors[1] * old[axis, layer - 1, t]
        part_y = factors[2] * north + factors[3] * south
        part_z = factors[4] * pltpu.roll(here, LANES - 1, 1) + factors[5] * pltpu.roll(here, 1, 1)
        change = ((source[axis, layer, t] - here) + part_x) + (part_y + part_z)
        value = here + sizes[level - 1] * change
        if level == SWEEPS:
            out_ref[axis, layer - HALO, pl.ds(t, ROWS, stride=TILES), :] = value
        else:
            new[axis, layer, t] = value

    def sweep_layer(level, layer, axes):
        old = field_at(level - 1)
        tiles = [[old[axis, layer, t] for t in range(TILES)] for axis in axes]
        for t in range(TILES):
            factors = [weights[layer, i, t] for i in range(6)]
            for axis, row in zip(axes, tiles):
                sweep_tile(level, layer, axis, t, row, factors)

    def sweep_inner(level, margin):
        def body(layer, carry):
            sweep_layer(level, layer, range(3))
            return carry

        lax.fori_loop(HALO + margin, HALO + LAYERS - margin, body, 0)

    def sweep_outer(level, margin, axis):
        for layer in range(margin - HALO, margin):
            sweep_layer(level, HALO + layer, [axis])
            sweep_layer(level, HALO + LAYERS - 1 - layer, [axis])

    for level in range(1, HALO + 1):
        sweep_inner(level, level)
    for copy in nu_copies:
        copy.wait_recv()

    def outer_weights(layer, carry):
        make_weights(layer)
        make_weights(layer + LAYERS + HALO - 2)
        return carry

    lax.fori_loop(1, HALO + 1, outer_weights, 0)

    def field_copies(axis):
        return [
            remote(field_a.at[axis, low], halo_high.at[axis], mid_send.at[0, axis], mid_recv.at[0, axis], below),
            remote(field_a.at[axis, high], halo_low.at[axis], mid_send.at[1, axis], mid_recv.at[1, axis], above),
        ]

    def first_outer(axis, carry):
        for copy in source_copies(axis):
            copy.wait()
        for layer in range(1, HALO + 1):
            scale_source(layer, axis)
            scale_source(layer + LAYERS + HALO - 2, axis)
        for level in range(1, HALO + 1):
            sweep_outer(level, level, axis)
        for copy in field_copies(axis):
            copy.start()
        return carry

    lax.fori_loop(0, 3, first_outer, 0)
    for level in range(1, HALO + 1):
        sweep_inner(HALO + level, level)

    def second_outer(axis, carry):
        for copy in field_copies(axis):
            copy.wait_recv()
        for layer in range(HALO):
            for t in range(TILES):
                field_a[axis, layer, t] = halo_low[axis, layer, t]
                field_a[axis, HALO + LAYERS + layer, t] = halo_high[axis, layer, t]
        for level in range(1, HALO + 1):
            sweep_outer(HALO + level, level, axis)
        return carry

    lax.fori_loop(0, 3, second_outer, 0)

    for copy in (pair, vel_up, vel_down, *nu_copies, *rs_copies, *ag_copies):
        copy.wait_send()

    def finish(at, carry):
        forward(at).wait_send()
        return carry

    lax.fori_loop(0, CHIPS, finish, 0)

    def finish_field(axis, carry):
        for copy in field_copies(axis):
            copy.wait_send()
        return carry

    lax.fori_loop(0, 3, finish_field, 0)


def per_device(velocity, forcing):
    f32 = jnp.float32
    full = LAYERS + 2 * HALO
    dma = pltpu.SemaphoreType.DMA
    tile = (ROWS, LANES)
    plane = (TILES * ROWS, LANES)
    result = pl.pallas_call(
        kernel,
        out_shape=jax.ShapeDtypeStruct(velocity.shape[1:], f32),
        in_specs=[pl.BlockSpec(memory_space=pltpu.MemorySpace.HBM)] * 2,
        out_specs=pl.BlockSpec(memory_space=pltpu.VMEM),
        scratch_shapes=[
            pltpu.VMEM((3, LAYERS + 2, *plane), f32),
            pltpu.VMEM((3, LAYERS, *plane), f32),
            pltpu.VMEM((3, CHIPS, *plane), f32),
            pltpu.VMEM((TILES, CHIPS, 4, *tile), f32),
            pltpu.VMEM((TILES, CHIPS, 4, *tile), f32),
            pltpu.VMEM((LAYERS, TILES, 4, *tile), f32),
            pltpu.VMEM((full, TILES, *tile), f32),
            pltpu.VMEM((full, 7, TILES, *tile), f32),
            pltpu.VMEM((3, full, TILES, *tile), f32),
            pltpu.VMEM((3, full, TILES, *tile), f32),
            pltpu.VMEM((3, full, TILES, *tile), f32),
            pltpu.VMEM((3, full, TILES, *tile), f32),
            pltpu.VMEM((3, HALO, TILES, *tile), f32),
            pltpu.VMEM((3, HALO, TILES, *tile), f32),
            dma((2,)), dma((2,)),
            dma((TILES, CHIPS)), dma((TILES, CHIPS)),
            dma((TILES, CHIPS)), dma((TILES, CHIPS)),
            dma((CHIPS,)), dma((CHIPS,)),
            dma((2,)), dma((2,)),
            dma((2,)), dma((2,)),
            dma((2, 3)), dma((2, 3)),
            dma((2, 3)), dma((2, 3)),
        ],
        compiler_params=pltpu.CompilerParams(
            collective_id=0, has_side_effects=True, vmem_limit_bytes=40 * 1024 * 1024
        ),
    )(
        pltpu.with_memory_space_constraint(velocity[0], pltpu.MemorySpace.HBM),
        pltpu.with_memory_space_constraint(forcing[0], pltpu.MemorySpace.HBM),
    )
    return result[None]


def solution(mesh):
    spec = P("member", None, "sub", None, None)
    return jax.shard_map(per_device, mesh=mesh, in_specs=(spec, spec), out_specs=spec, check_vma=False)
```

```python
import functools
import math

import jax
import jax.numpy as jnp
from jax import lax
from jax.experimental import pallas as pl
from jax.experimental.pallas import tpu as pltpu
from jax.sharding import PartitionSpec as P

MESH = pl.DeviceIdType.MESH
SWEEPS = 8
TIME_STEP = 0.25
EDDY_COEFF = 1.0
BASE_VISCOSITY = 1.0
LOWER_EDGE = 0.1
UPPER_EDGE = 1.9

LAYERS = 16
TILES = 4
ROWS = 8
LANES = 128
CHIPS = 8
HALO = 4
PARTS = 4
SPAN = TILES // PARTS
ORDER = ((2, 1), (1, 1), (3, 1), (2, 0), (1, 0), (3, 0), (0, 1))


def step_sizes(sweep_count):
    middle = (UPPER_EDGE + LOWER_EDGE) / 2
    radius = (UPPER_EDGE - LOWER_EDGE) / 2
    return [
        1.0 / (middle + radius * math.cos(math.pi * (2 * position + 1) / (2 * sweep_count)))
        for position in range(sweep_count)
    ]


def shifted_chip(chip, dx, dy):
    x, y = chip // 2, lax.rem(chip, 2)
    return lax.rem(x + dx, 4) * 2 + lax.rem(y + dy, 2)


def kernel(
    vel_ref, force_ref, out_ref,
    vel, force, partner_vel, sums, arrived, flow, pre, slopes, nu, weights, source, field_a, field_b, field_c, halo_low, halo_high,
    load_sem, pair_sem, rs_send, rs_recv, ag_send, ag_recv, fw_send, fw_recv,
    vh_send, vh_recv, nu_send, nu_recv, src_send, src_recv, mid_send, mid_recv,
):
    member, sub = lax.axis_index("member"), lax.axis_index("sub")
    chip, core = member // 2, lax.rem(member, 2)
    subs = lax.axis_size("sub")
    above = (member, lax.rem(sub + 1, subs))
    below = (member, lax.rem(sub + subs - 1, subs))
    partner = (chip * 2 + 1 - core, sub)
    peers = [(shifted_chip(chip, dx, dy) * 2 + core, sub) for dx, dy in ORDER]
    targets = [shifted_chip(chip, dx, dy) for dx, dy in ORDER]
    origins = [shifted_chip(chip, 4 - dx, dy) for dx, dy in ORDER]

    def remote(src, dst, send, recv, device):
        return pltpu.make_async_remote_copy(
            src_ref=src, dst_ref=dst, send_sem=send, recv_sem=recv, device_id=device, device_id_type=MESH
        )

    load_vel = pltpu.make_async_copy(vel_ref, vel.at[:, pl.ds(1, LAYERS)], load_sem.at[0])
    load_force = pltpu.make_async_copy(force_ref, force, load_sem.at[1])
    load_vel.start()
    load_force.start()

    barrier = pltpu.get_barrier_semaphore()
    greeted = [*peers, partner, above, below]
    for device in greeted:
        pl.semaphore_signal(barrier, inc=1, device_id=device, device_id_type=MESH)
    pl.semaphore_wait(barrier, len(greeted))

    pair = remote(
        vel_ref.at[:, pl.ds((1 - core) * CHIPS, CHIPS)], partner_vel, pair_sem.at[0], pair_sem.at[1], partner
    )
    pair.start()
    load_vel.wait()
    pair.wait_recv()

    vel_up = remote(vel_ref.at[:, LAYERS - 1], vel.at[:, 0], vh_send.at[0], vh_recv.at[0], above)
    vel_down = remote(vel_ref.at[:, 0], vel.at[:, LAYERS + 1], vh_send.at[1], vh_recv.at[1], below)

    def tile_rows(t):
        return pl.ds(t, ROWS, stride=TILES)

    def pair_sums(part, target):
        for k in range(SPAN):
            rows = tile_rows(part * SPAN + k)
            squares = None
            for axis in range(3):
                mine = vel[axis, 1 + core * CHIPS + target, rows, :]
                other = partner_vel[axis, target, rows, :]
                sums[part, target, k, axis] = mine + other
                term = mine * mine + other * other
                squares = term if squares is None else squares + term
            sums[part, target, k, 3] = squares

    for part in range(PARTS):
        for target in targets:
            pair_sums(part, target)
        pair_sums(part, chip)
        for place, target in enumerate(targets):
            remote(
                sums.at[part, target], arrived.at[part, chip], rs_send.at[0], rs_recv.at[part], peers[place]
            ).start()
    vel_up.start()
    vel_down.start()

    others = pl.ds(0, CHIPS - 1)
    own = core * CHIPS + chip
    for part in range(PARTS):
        remote(
            sums.at[part, others], arrived.at[part, others], rs_send.at[0], rs_recv.at[part], partner
        ).wait_recv()
        for k in range(SPAN):
            tile = part * SPAN + k
            total = [
                (
                    (sums[part, chip, k, i] + arrived[part, origins[0], k, i])
                    + (arrived[part, origins[1], k, i] + arrived[part, origins[2], k, i])
                )
                + (
                    (arrived[part, origins[3], k, i] + arrived[part, origins[4], k, i])
                    + (arrived[part, origins[5], k, i] + arrived[part, origins[6], k, i])
                )
                for i in range(4)
            ]
            mean = [total[i] * (1.0 / 16) for i in range(3)]
            spread = total[3] * (1.0 / 16) - (mean[0] * mean[0] + mean[1] * mean[1] + mean[2] * mean[2])
            for i in range(3):
                flow[own, tile, i] = mean[i]
            flow[own, tile, 3] = BASE_VISCOSITY + EDDY_COEFF * TIME_STEP * spread
        piece = flow.at[own, pl.ds(part * SPAN, SPAN)]
        for peer in peers:
            remote(piece, piece, ag_send.at[0], ag_recv.at[chip], peer).start()

    load_force.wait()
    vel_up.wait_recv()
    vel_down.wait_recv()

    def prepare(layer, carry):
        for axis in range(3):
            tiles = [vel[axis, layer + 1, tile_rows(t), :] for t in range(TILES)]
            for t in range(TILES):
                here = tiles[t]
                north = tiles[t + 1] if t + 1 < TILES else pltpu.roll(tiles[0], ROWS - 1, 0)
                south = tiles[t - 1] if t > 0 else pltpu.roll(tiles[TILES - 1], 1, 0)
                gaps = (
                    vel[axis, layer, tile_rows(t), :] - vel[axis, layer + 2, tile_rows(t), :],
                    south - north,
                    pltpu.roll(here, 1, 1) - pltpu.roll(here, LANES - 1, 1),
                )
                for i in range(3):
                    slopes[layer, axis, i, t] = (0.5 * TIME_STEP) * gaps[i]
                pre[layer, axis, t] = here + TIME_STEP * force[axis, layer, tile_rows(t), :]
        return carry

    lax.fori_loop(0, LAYERS, prepare, 0)

    def make_source(layer):
        for t in range(TILES):
            mean = [flow[layer, t, i] for i in range(3)]
            nu[HALO + layer, t] = flow[layer, t, 3]
            for axis in range(3):
                moved = mean[0] * slopes[layer, axis, 0, t] + mean[1] * slopes[layer, axis, 1, t]
                field_a[axis, HALO + layer, t] = pre[layer, axis, t] + (moved + mean[2] * slopes[layer, axis, 2, t])

    def chip_at(k):
        return shifted_chip(chip, k // 2, lax.rem(k, 2))

    def forward(at):
        layer = core * CHIPS + at
        return remote(flow.at[layer], flow.at[layer], fw_send.at[0], fw_recv.at[at], partner)

    forward(chip).start()
    make_source(own)

    def gather_step(k, carry):
        @pl.when(k < CHIPS)
        def _():
            at = chip_at(k)
            layer = core * CHIPS + at
            remote(flow.at[layer], flow.at[layer], ag_send.at[0], ag_recv.at[at], partner).wait_recv()
            forward(at).start()
            make_source(layer)

        at = chip_at(k - 1)
        layer = (1 - core) * CHIPS + at
        remote(flow.at[layer], flow.at[layer], fw_send.at[0], fw_recv.at[at], partner).wait_recv()
        make_source(layer)
        return carry

    lax.fori_loop(1, CHIPS + 1, gather_step, 0)

    low, high = pl.ds(HALO, HALO), pl.ds(LAYERS, HALO)
    before, after = pl.ds(0, HALO), pl.ds(HALO + LAYERS, HALO)
    nu_copies = [
        remote(nu.at[low], nu.at[after], nu_send.at[0], nu_recv.at[0], below),
        remote(nu.at[high], nu.at[before], nu_send.at[1], nu_recv.at[1], above),
    ]
    for copy in nu_copies:
        copy.start()

    def source_copies(axis):
        return [
            remote(
                field_a.at[axis, low], field_a.at[axis, after], src_send.at[0, axis], src_recv.at[0, axis], below
            ),
            remote(
                field_a.at[axis, high], field_a.at[axis, before], src_send.at[1, axis], src_recv.at[1, axis], above
            ),
        ]

    for axis in range(3):
        for copy in source_copies(axis):
            copy.start()

    def make_weights(layer):
        centre = [nu[layer, t] for t in range(TILES)]
        for t in range(TILES):
            here = centre[t]
            north = centre[t + 1] if t + 1 < TILES else pltpu.roll(centre[0], ROWS - 1, 0)
            south = centre[t - 1] if t > 0 else pltpu.roll(centre[TILES - 1], 1, 0)
            around = (
                nu[layer + 1, t], nu[layer - 1, t], north, south,
                pltpu.roll(here, LANES - 1, 1), pltpu.roll(here, 1, 1),
            )
            faces = [here + other for other in around]
            total = ((faces[0] + faces[1]) + (faces[2] + faces[3])) + (faces[4] + faces[5])
            inverse = 1.0 / (1.0 + (0.5 * TIME_STEP) * total)
            scaled = (0.5 * TIME_STEP) * inverse
            for i in range(6):
                weights[layer, i, t] = faces[i] * scaled
            weights[layer, 6, t] = inverse

    def scale_source(layer, axis):
        for t in range(TILES):
            source[axis, layer, t] = field_a[axis, layer, t] * weights[layer, 6, t]

    def inner_weights(layer, carry):
        make_weights(layer)
        for axis in range(3):
            scale_source(layer, axis)
        return carry

    lax.fori_loop(HALO + 1, HALO + LAYERS - 1, inner_weights, 0)

    sizes = step_sizes(SWEEPS)

    def field_at(level):
        if level % HALO == 0:
            return field_a
        return (field_c, field_b)[level % 2]

    def sweep_tile(level, layer, axis, t, tiles, factors):
        old, new = field_at(level - 1), field_at(level)
        here = tiles[t]
        north = tiles[t + 1] if t + 1 < TILES else pltpu.roll(tiles[0], ROWS - 1, 0)
        south = tiles[t - 1] if t > 0 else pltpu.roll(tiles[TILES - 1], 1, 0)
        part_x = factors[0] * old[axis, layer + 1, t] + factors[1] * old[axis, layer - 1, t]
        part_y = factors[2] * north + factors[3] * south
        part_z = factors[4] * pltpu.roll(here, LANES - 1, 1) + factors[5] * pltpu.roll(here, 1, 1)
        change = ((source[axis, layer, t] - here) + part_x) + (part_y + part_z)
        value = here + sizes[level - 1] * change
        if level == SWEEPS:
            out_ref[axis, layer - HALO, pl.ds(t, ROWS, stride=TILES), :] = value
        else:
            new[axis, layer, t] = value

    def sweep_layer(level, layer, axes):
        old = field_at(level - 1)
        tiles = [[old[axis, layer, t] for t in range(TILES)] for axis in axes]
        for t in range(TILES):
            factors = [weights[layer, i, t] for i in range(6)]
            for axis, row in zip(axes, tiles):
                sweep_tile(level, layer, axis, t, row, factors)

    def sweep_inner(level, margin):
        def body(i, carry):
            for k in range(2):
                sweep_layer(level, HALO + margin + 2 * i + k, range(3))
            return carry

        lax.fori_loop(0, LAYERS // 2 - margin, body, 0)

    def sweep_outer(level, margin, axis):
        for layer in range(margin - HALO, margin):
            sweep_layer(level, HALO + layer, [axis])
            sweep_layer(level, HALO + LAYERS - 1 - layer, [axis])

    for level in range(1, HALO + 1):
        sweep_inner(level, level)
    for copy in (pair, vel_up, vel_down):
        copy.wait_send()
    remote(sums.at[:, others], arrived.at[:, others], rs_send.at[0], rs_recv.at[0], partner).wait_send()
    remote(sums.at[:, others], arrived.at[:, others], ag_send.at[0], ag_recv.at[0], partner).wait_send()
    half = pl.ds(0, CHIPS)
    remote(flow.at[half], flow.at[half], fw_send.at[0], fw_recv.at[0], partner).wait_send()
    for copy in nu_copies:
        copy.wait()

    def outer_weights(layer, carry):
        make_weights(layer)
        make_weights(layer + LAYERS + HALO - 2)
        return carry

    lax.fori_loop(1, HALO + 1, outer_weights, 0)

    def field_copies(axis):
        return [
            remote(field_a.at[axis, low], halo_high.at[axis], mid_send.at[0, axis], mid_recv.at[0, axis], below),
            remote(field_a.at[axis, high], halo_low.at[axis], mid_send.at[1, axis], mid_recv.at[1, axis], above),
        ]

    def first_outer(axis, carry):
        for copy in source_copies(axis):
            copy.wait()
        for layer in range(1, HALO + 1):
            scale_source(layer, axis)
            scale_source(layer + LAYERS + HALO - 2, axis)
        for level in range(1, HALO + 1):
            sweep_outer(level, level, axis)
        for copy in field_copies(axis):
            copy.start()
        return carry

    lax.fori_loop(0, 3, first_outer, 0)
    for level in range(1, HALO + 1):
        sweep_inner(HALO + level, level)

    def second_outer(axis, carry):
        for copy in field_copies(axis):
            copy.wait_recv()
        for layer in range(HALO):
            for t in range(TILES):
                field_a[axis, layer, t] = halo_low[axis, layer, t]
                field_a[axis, HALO + LAYERS + layer, t] = halo_high[axis, layer, t]
        for level in range(1, HALO + 1):
            sweep_outer(HALO + level, level, axis)
        return carry

    lax.fori_loop(0, 3, second_outer, 0)

    def finish_field(axis, carry):
        for copy in field_copies(axis):
            copy.wait_send()
        return carry

    lax.fori_loop(0, 3, finish_field, 0)


def per_device(velocity, forcing):
    f32 = jnp.float32
    full = LAYERS + 2 * HALO
    dma = pltpu.SemaphoreType.DMA
    tile = (ROWS, LANES)
    plane = (TILES * ROWS, LANES)
    result = pl.pallas_call(
        kernel,
        out_shape=jax.ShapeDtypeStruct(velocity.shape[1:], f32),
        in_specs=[pl.BlockSpec(memory_space=pltpu.MemorySpace.HBM)] * 2,
        out_specs=pl.BlockSpec(memory_space=pltpu.VMEM),
        scratch_shapes=[
            pltpu.VMEM((3, LAYERS + 2, *plane), f32),
            pltpu.VMEM((3, LAYERS, *plane), f32),
            pltpu.VMEM((3, CHIPS, *plane), f32),
            pltpu.VMEM((PARTS, CHIPS, SPAN, 4, *tile), f32),
            pltpu.VMEM((PARTS, CHIPS, SPAN, 4, *tile), f32),
            pltpu.VMEM((LAYERS, TILES, 4, *tile), f32),
            pltpu.VMEM((LAYERS, 3, TILES, *tile), f32),
            pltpu.VMEM((LAYERS, 3, 3, TILES, *tile), f32),
            pltpu.VMEM((full, TILES, *tile), f32),
            pltpu.VMEM((full, 7, TILES, *tile), f32),
            pltpu.VMEM((3, full, TILES, *tile), f32),
            pltpu.VMEM((3, full, TILES, *tile), f32),
            pltpu.VMEM((3, full, TILES, *tile), f32),
            pltpu.VMEM((3, full, TILES, *tile), f32),
            pltpu.VMEM((3, HALO, TILES, *tile), f32),
            pltpu.VMEM((3, HALO, TILES, *tile), f32),
            dma((2,)), dma((2,)),
            dma((1,)), dma((PARTS,)),
            dma((1,)), dma((CHIPS,)),
            dma((1,)), dma((CHIPS,)),
            dma((2,)), dma((2,)),
            dma((2,)), dma((2,)),
            dma((2, 3)), dma((2, 3)),
            dma((2, 3)), dma((2, 3)),
        ],
        compiler_params=pltpu.CompilerParams(
            collective_id=0, has_side_effects=True, vmem_limit_bytes=40 * 1024 * 1024
        ),
    )(
        pltpu.with_memory_space_constraint(velocity[0], pltpu.MemorySpace.HBM),
        pltpu.with_memory_space_constraint(forcing[0], pltpu.MemorySpace.HBM),
    )
    return result[None]


def solution(mesh):
    spec = P("member", None, "sub", None, None)
    return jax.shard_map(per_device, mesh=mesh, in_specs=(spec, spec), out_specs=spec, check_vma=False)
```

```python
import functools
import math

import jax
import jax.numpy as jnp
from jax import lax
from jax.experimental import pallas as pl
from jax.experimental.pallas import tpu as pltpu
from jax.sharding import PartitionSpec as P

MESH = pl.DeviceIdType.MESH
SWEEPS = 8
TIME_STEP = 0.25
EDDY_COEFF = 1.0
BASE_VISCOSITY = 1.0
LOWER_EDGE = 0.1
UPPER_EDGE = 1.9

LAYERS = 16
TILES = 4
ROWS = 8
LANES = 128
CHIPS = 8
HALO = 4
PARTS = 4
ORDER = ((2, 1), (1, 1), (3, 1), (2, 0), (1, 0), (3, 0), (0, 1))


def step_sizes(sweep_count):
    middle = (UPPER_EDGE + LOWER_EDGE) / 2
    radius = (UPPER_EDGE - LOWER_EDGE) / 2
    return [
        1.0 / (middle + radius * math.cos(math.pi * (2 * position + 1) / (2 * sweep_count)))
        for position in range(sweep_count)
    ]


def shifted_chip(chip, dx, dy):
    x, y = chip // 2, lax.rem(chip, 2)
    return lax.rem(x + dx, 4) * 2 + lax.rem(y + dy, 2)


def kernel(
    vel_ref, force_ref, out_ref,
    vel, force, partner_vel, sums, arrived, flow, pre, slopes, nu, weights, source, field_a, field_b, field_c, halo_low, halo_high,
    load_sem, pair_sem, rs_send, rs_recv, ag_send, ag_recv, fw_send, fw_recv,
    vh_send, vh_recv, nu_send, nu_recv, src_send, src_recv, mid_send, mid_recv,
):
    member, sub = lax.axis_index("member"), lax.axis_index("sub")
    chip, core = member // 2, lax.rem(member, 2)
    subs = lax.axis_size("sub")
    above = (member, lax.rem(sub + 1, subs))
    below = (member, lax.rem(sub + subs - 1, subs))
    partner = (chip * 2 + 1 - core, sub)
    peers = [(shifted_chip(chip, dx, dy) * 2 + core, sub) for dx, dy in ORDER]
    targets = [shifted_chip(chip, dx, dy) for dx, dy in ORDER]
    origins = [shifted_chip(chip, 4 - dx, dy) for dx, dy in ORDER]

    def remote(src, dst, send, recv, device):
        return pltpu.make_async_remote_copy(
            src_ref=src, dst_ref=dst, send_sem=send, recv_sem=recv, device_id=device, device_id_type=MESH
        )

    load_vel = pltpu.make_async_copy(vel_ref, vel.at[:, pl.ds(1, LAYERS)], load_sem.at[0])
    load_force = pltpu.make_async_copy(force_ref, force, load_sem.at[1])
    load_vel.start()
    load_force.start()

    barrier = pltpu.get_barrier_semaphore()
    greeted = [*peers, partner, above, below]
    for device in greeted:
        pl.semaphore_signal(barrier, inc=1, device_id=device, device_id_type=MESH)
    pl.semaphore_wait(barrier, len(greeted))

    def part_rows(part):
        return pl.ds(part * ROWS, ROWS)

    pairs = [
        remote(
            vel_ref.at[:, pl.ds((1 - core) * CHIPS, CHIPS), part_rows(part)], partner_vel.at[:, :, part_rows(part)],
            pair_sem.at[0, part], pair_sem.at[1, part], partner,
        )
        for part in range(PARTS)
    ]
    for copy in pairs:
        copy.start()

    vel_up = remote(vel_ref.at[:, LAYERS - 1], vel.at[:, 0], vh_send.at[0], vh_recv.at[0], above)
    vel_down = remote(vel_ref.at[:, 0], vel.at[:, LAYERS + 1], vh_send.at[1], vh_recv.at[1], below)

    def tile_rows(t):
        return pl.ds(t, ROWS, stride=TILES)

    def pair_sums(part, target):
        squares = None
        for axis in range(3):
            mine = vel[axis, 1 + core * CHIPS + target, part_rows(part), :]
            other = partner_vel[axis, target, part_rows(part), :]
            sums[part, target, axis] = mine + other
            term = mine * mine + other * other
            squares = term if squares is None else squares + term
        sums[part, target, 3] = squares

    load_vel.wait()
    for part in range(PARTS):
        pairs[part].wait_recv()
        for target in targets:
            pair_sums(part, target)
        pair_sums(part, chip)
        for place, target in enumerate(targets):
            remote(
                sums.at[part, target], arrived.at[part, chip], rs_send.at[0], rs_recv.at[part], peers[place]
            ).start()
    vel_up.start()
    vel_down.start()

    others = pl.ds(0, CHIPS - 1)
    own = core * CHIPS + chip
    for part in range(PARTS):
        remote(
            sums.at[part, others], arrived.at[part, others], rs_send.at[0], rs_recv.at[part], partner
        ).wait_recv()
        total = [
            (
                (sums[part, chip, i] + arrived[part, origins[0], i])
                + (arrived[part, origins[1], i] + arrived[part, origins[2], i])
            )
            + (
                (arrived[part, origins[3], i] + arrived[part, origins[4], i])
                + (arrived[part, origins[5], i] + arrived[part, origins[6], i])
            )
            for i in range(4)
        ]
        mean = [total[i] * (1.0 / 16) for i in range(3)]
        spread = total[3] * (1.0 / 16) - (mean[0] * mean[0] + mean[1] * mean[1] + mean[2] * mean[2])
        for i in range(3):
            flow[own, i, part_rows(part), :] = mean[i]
        flow[own, 3, part_rows(part), :] = BASE_VISCOSITY + EDDY_COEFF * TIME_STEP * spread
        piece = flow.at[own, :, part_rows(part)]
        for peer in peers:
            remote(piece, piece, ag_send.at[0], ag_recv.at[chip], peer).start()

    load_force.wait()
    vel_up.wait_recv()
    vel_down.wait_recv()

    def prepare(layer, carry):
        for axis in range(3):
            tiles = [vel[axis, layer + 1, tile_rows(t), :] for t in range(TILES)]
            for t in range(TILES):
                here = tiles[t]
                north = tiles[t + 1] if t + 1 < TILES else pltpu.roll(tiles[0], ROWS - 1, 0)
                south = tiles[t - 1] if t > 0 else pltpu.roll(tiles[TILES - 1], 1, 0)
                gaps = (
                    vel[axis, layer, tile_rows(t), :] - vel[axis, layer + 2, tile_rows(t), :],
                    south - north,
                    pltpu.roll(here, 1, 1) - pltpu.roll(here, LANES - 1, 1),
                )
                for i in range(3):
                    slopes[layer, axis, i, t] = (0.5 * TIME_STEP) * gaps[i]
                pre[layer, axis, t] = here + TIME_STEP * force[axis, layer, tile_rows(t), :]
        return carry

    lax.fori_loop(0, LAYERS, prepare, 0)

    def make_source(layer):
        for t in range(TILES):
            mean = [flow[layer, i, tile_rows(t), :] for i in range(3)]
            nu[HALO + layer, t] = flow[layer, 3, tile_rows(t), :]
            for axis in range(3):
                moved = mean[0] * slopes[layer, axis, 0, t] + mean[1] * slopes[layer, axis, 1, t]
                field_a[axis, HALO + layer, t] = pre[layer, axis, t] + (moved + mean[2] * slopes[layer, axis, 2, t])

    def chip_at(k):
        return shifted_chip(chip, k // 2, lax.rem(k, 2))

    def forward(at):
        layer = core * CHIPS + at
        return remote(flow.at[layer], flow.at[layer], fw_send.at[0], fw_recv.at[at], partner)

    forward(chip).start()

    def gather_step(k, carry):
        at = chip_at(k)
        layer = core * CHIPS + at
        remote(flow.at[layer], flow.at[layer], ag_send.at[0], ag_recv.at[at], partner).wait_recv()
        forward(at).start()
        return carry

    lax.fori_loop(1, CHIPS, gather_step, 0)

    def direct_sources(first):
        def body(i, carry):
            make_source(first + i)
            return carry

        lax.fori_loop(0, HALO, body, 0)

    def forwarded_sources(first):
        def body(i, carry):
            at = first + i - (1 - core) * CHIPS
            forward(at).wait_recv()
            make_source(first + i)
            return carry

        lax.fori_loop(0, HALO, body, 0)

    low, high = pl.ds(HALO, HALO), pl.ds(LAYERS, HALO)

    def side_of(side):
        device = (member, jnp.where(side == 1, above[1], below[1]))
        return (
            pl.ds(jnp.where(side == 1, LAYERS, HALO), HALO),
            pl.ds(jnp.where(side == 1, 0, HALO + LAYERS), HALO),
            device,
        )

    def nu_copy(side):
        inside, outside, device = side_of(side)
        return remote(nu.at[inside], nu.at[outside], nu_send.at[side], nu_recv.at[side], device)

    def source_copy(side, axis):
        inside, outside, device = side_of(side)
        return remote(
            field_a.at[axis, inside], field_a.at[axis, outside], src_send.at[side, axis], src_recv.at[side, axis],
            device,
        )

    def send_side(side):
        nu_copy(side).start()
        for axis in range(3):
            source_copy(side, axis).start()

    direct_sources(core * (LAYERS - HALO))
    send_side(core)
    forwarded_sources((1 - core) * (LAYERS - HALO))
    send_side(1 - core)
    direct_sources(HALO + core * HALO)
    forwarded_sources(HALO + (1 - core) * HALO)

    def make_weights(layer):
        centre = [nu[layer, t] for t in range(TILES)]
        for t in range(TILES):
            here = centre[t]
            north = centre[t + 1] if t + 1 < TILES else pltpu.roll(centre[0], ROWS - 1, 0)
            south = centre[t - 1] if t > 0 else pltpu.roll(centre[TILES - 1], 1, 0)
            around = (
                nu[layer + 1, t], nu[layer - 1, t], north, south,
                pltpu.roll(here, LANES - 1, 1), pltpu.roll(here, 1, 1),
            )
            faces = [here + other for other in around]
            total = ((faces[0] + faces[1]) + (faces[2] + faces[3])) + (faces[4] + faces[5])
            inverse = 1.0 / (1.0 + (0.5 * TIME_STEP) * total)
            scaled = (0.5 * TIME_STEP) * inverse
            for i in range(6):
                weights[layer, i, t] = faces[i] * scaled
            weights[layer, 6, t] = inverse

    def scale_source(layer, axis):
        for t in range(TILES):
            source[axis, layer, t] = field_a[axis, layer, t] * weights[layer, 6, t]

    def inner_weights(layer, carry):
        make_weights(layer)
        for axis in range(3):
            scale_source(layer, axis)
        return carry

    lax.fori_loop(HALO + 1, HALO + LAYERS - 1, inner_weights, 0)

    sizes = step_sizes(SWEEPS)

    def field_at(level):
        if level % HALO == 0:
            return field_a
        return (field_c, field_b)[level % 2]

    def sweep_tile(level, layer, axis, t, tiles, factors):
        old, new = field_at(level - 1), field_at(level)
        here = tiles[t]
        north = tiles[t + 1] if t + 1 < TILES else pltpu.roll(tiles[0], ROWS - 1, 0)
        south = tiles[t - 1] if t > 0 else pltpu.roll(tiles[TILES - 1], 1, 0)
        part_x = factors[0] * old[axis, layer + 1, t] + factors[1] * old[axis, layer - 1, t]
        part_y = factors[2] * north + factors[3] * south
        part_z = factors[4] * pltpu.roll(here, LANES - 1, 1) + factors[5] * pltpu.roll(here, 1, 1)
        change = ((source[axis, layer, t] - here) + part_x) + (part_y + part_z)
        value = here + sizes[level - 1] * change
        if level == SWEEPS:
            out_ref[axis, layer - HALO, pl.ds(t, ROWS, stride=TILES), :] = value
        else:
            new[axis, layer, t] = value

    def sweep_layer(level, layer, axes):
        old = field_at(level - 1)
        tiles = [[old[axis, layer, t] for t in range(TILES)] for axis in axes]
        for t in range(TILES):
            factors = [weights[layer, i, t] for i in range(6)]
            for axis, row in zip(axes, tiles):
                sweep_tile(level, layer, axis, t, row, factors)

    def sweep_inner(level, margin):
        def body(i, carry):
            for k in range(2):
                sweep_layer(level, HALO + margin + 2 * i + k, range(3))
            return carry

        lax.fori_loop(0, LAYERS // 2 - margin, body, 0)

    def sweep_outer(level, margin, axis):
        for layer in range(margin - HALO, margin):
            sweep_layer(level, HALO + layer, [axis])
            sweep_layer(level, HALO + LAYERS - 1 - layer, [axis])

    for level in range(1, HALO + 1):
        sweep_inner(level, level)
    for copy in (*pairs, vel_up, vel_down):
        copy.wait_send()
    remote(sums.at[:, others], arrived.at[:, others], rs_send.at[0], rs_recv.at[0], partner).wait_send()
    remote(sums.at[:, others], arrived.at[:, others], ag_send.at[0], ag_recv.at[0], partner).wait_send()
    half = pl.ds(0, CHIPS)
    remote(flow.at[half], flow.at[half], fw_send.at[0], fw_recv.at[0], partner).wait_send()
    for side in range(2):
        nu_copy(side).wait()

    def outer_weights(layer, carry):
        make_weights(layer)
        make_weights(layer + LAYERS + HALO - 2)
        return carry

    lax.fori_loop(1, HALO + 1, outer_weights, 0)

    def field_copies(axis):
        return [
            remote(field_a.at[axis, low], halo_high.at[axis], mid_send.at[0, axis], mid_recv.at[0, axis], below),
            remote(field_a.at[axis, high], halo_low.at[axis], mid_send.at[1, axis], mid_recv.at[1, axis], above),
        ]

    def first_outer(axis, carry):
        for side in range(2):
            source_copy(side, axis).wait()
        for layer in range(1, HALO + 1):
            scale_source(layer, axis)
            scale_source(layer + LAYERS + HALO - 2, axis)
        for level in range(1, HALO + 1):
            sweep_outer(level, level, axis)
        for copy in field_copies(axis):
            copy.start()
        return carry

    lax.fori_loop(0, 3, first_outer, 0)
    for level in range(1, HALO + 1):
        sweep_inner(HALO + level, level)

    def second_outer(axis, carry):
        for copy in field_copies(axis):
            copy.wait_recv()
        for layer in range(HALO):
            for t in range(TILES):
                field_a[axis, layer, t] = halo_low[axis, layer, t]
                field_a[axis, HALO + LAYERS + layer, t] = halo_high[axis, layer, t]
        for level in range(1, HALO + 1):
            sweep_outer(HALO + level, level, axis)
        return carry

    lax.fori_loop(0, 3, second_outer, 0)

    def finish_field(axis, carry):
        for copy in field_copies(axis):
            copy.wait_send()
        return carry

    lax.fori_loop(0, 3, finish_field, 0)


def per_device(velocity, forcing):
    f32 = jnp.float32
    full = LAYERS + 2 * HALO
    dma = pltpu.SemaphoreType.DMA
    tile = (ROWS, LANES)
    plane = (TILES * ROWS, LANES)
    result = pl.pallas_call(
        kernel,
        out_shape=jax.ShapeDtypeStruct(velocity.shape[1:], f32),
        in_specs=[pl.BlockSpec(memory_space=pltpu.MemorySpace.HBM)] * 2,
        out_specs=pl.BlockSpec(memory_space=pltpu.VMEM),
        scratch_shapes=[
            pltpu.VMEM((3, LAYERS + 2, *plane), f32),
            pltpu.VMEM((3, LAYERS, *plane), f32),
            pltpu.VMEM((3, CHIPS, *plane), f32),
            pltpu.VMEM((PARTS, CHIPS, 4, *tile), f32),
            pltpu.VMEM((PARTS, CHIPS, 4, *tile), f32),
            pltpu.VMEM((LAYERS, 4, *plane), f32),
            pltpu.VMEM((LAYERS, 3, TILES, *tile), f32),
            pltpu.VMEM((LAYERS, 3, 3, TILES, *tile), f32),
            pltpu.VMEM((full, TILES, *tile), f32),
            pltpu.VMEM((full, 7, TILES, *tile), f32),
            pltpu.VMEM((3, full, TILES, *tile), f32),
            pltpu.VMEM((3, full, TILES, *tile), f32),
            pltpu.VMEM((3, full, TILES, *tile), f32),
            pltpu.VMEM((3, full, TILES, *tile), f32),
            pltpu.VMEM((3, HALO, TILES, *tile), f32),
            pltpu.VMEM((3, HALO, TILES, *tile), f32),
            dma((2,)), dma((2, PARTS)),
            dma((1,)), dma((PARTS,)),
            dma((1,)), dma((CHIPS,)),
            dma((1,)), dma((CHIPS,)),
            dma((2,)), dma((2,)),
            dma((2,)), dma((2,)),
            dma((2, 3)), dma((2, 3)),
            dma((2, 3)), dma((2, 3)),
        ],
        compiler_params=pltpu.CompilerParams(
            collective_id=0, has_side_effects=True, vmem_limit_bytes=40 * 1024 * 1024
        ),
    )(
        pltpu.with_memory_space_constraint(velocity[0], pltpu.MemorySpace.HBM),
        pltpu.with_memory_space_constraint(forcing[0], pltpu.MemorySpace.HBM),
    )
    return result[None]


def solution(mesh):
    spec = P("member", None, "sub", None, None)
    return jax.shard_map(per_device, mesh=mesh, in_specs=(spec, spec), out_specs=spec, check_vma=False)
```

```python
import functools
import math

import jax
import jax.numpy as jnp
from jax import lax
from jax.experimental import pallas as pl
from jax.experimental.pallas import tpu as pltpu
from jax.sharding import PartitionSpec as P

MESH = pl.DeviceIdType.MESH
SWEEPS = 8
TIME_STEP = 0.25
EDDY_COEFF = 1.0
BASE_VISCOSITY = 1.0
LOWER_EDGE = 0.1
UPPER_EDGE = 1.9

LAYERS = 16
TILES = 4
ROWS = 8
LANES = 128
CHIPS = 8
HALO = 4
PARTS = 4
ORDER = ((2, 1), (1, 1), (3, 1), (2, 0), (1, 0), (3, 0), (0, 1))


def step_sizes(sweep_count):
    middle = (UPPER_EDGE + LOWER_EDGE) / 2
    radius = (UPPER_EDGE - LOWER_EDGE) / 2
    return [
        1.0 / (middle + radius * math.cos(math.pi * (2 * position + 1) / (2 * sweep_count)))
        for position in range(sweep_count)
    ]


def shifted_chip(chip, dx, dy):
    x, y = chip // 2, lax.rem(chip, 2)
    return lax.rem(x + dx, 4) * 2 + lax.rem(y + dy, 2)


def kernel(
    vel_ref, force_ref, out_ref,
    vel, force, partner_vel, sums, arrived, flow, pre, slopes, nu, weights, source, field_a, field_b, field_c, halo_low, halo_high,
    load_sem, pair_send, pair_recv, rs_send, rs_recv, ag_send, ag_recv, fw_send, fw_recv,
    vh_send, vh_recv, nu_send, nu_recv, src_send, src_recv, mid_send, mid_recv,
):
    member, sub = lax.axis_index("member"), lax.axis_index("sub")
    chip, core = member // 2, lax.rem(member, 2)
    subs = lax.axis_size("sub")
    above = (member, lax.rem(sub + 1, subs))
    below = (member, lax.rem(sub + subs - 1, subs))
    partner = (chip * 2 + 1 - core, sub)
    peers = [(shifted_chip(chip, dx, dy) * 2 + core, sub) for dx, dy in ORDER]
    targets = [shifted_chip(chip, dx, dy) for dx, dy in ORDER]
    origins = [shifted_chip(chip, 4 - dx, dy) for dx, dy in ORDER]

    def remote(src, dst, send, recv, device):
        return pltpu.make_async_remote_copy(
            src_ref=src, dst_ref=dst, send_sem=send, recv_sem=recv, device_id=device, device_id_type=MESH
        )

    def load_half(half):
        return pltpu.make_async_copy(
            vel_ref.at[:, pl.ds(half * CHIPS, CHIPS)], vel.at[:, pl.ds(1 + half * CHIPS, CHIPS)], load_sem.at[half]
        )

    load_force = pltpu.make_async_copy(force_ref, force, load_sem.at[2])
    load_half(core).start()
    load_half(1 - core).start()
    load_force.start()

    barrier = pltpu.get_barrier_semaphore()
    greeted = [*peers, partner, above, below]
    for device in greeted:
        pl.semaphore_signal(barrier, inc=1, device_id=device, device_id_type=MESH)
    pl.semaphore_wait(barrier, len(greeted))

    def part_rows(part):
        return pl.ds(part * ROWS, ROWS)

    pairs = [
        remote(
            vel_ref.at[:, pl.ds((1 - core) * CHIPS, CHIPS), part_rows(part)], partner_vel.at[:, :, part_rows(part)],
            pair_send.at[0], pair_recv.at[part], partner,
        )
        for part in range(PARTS)
    ]
    for copy in pairs:
        copy.start()

    def tile_rows(t):
        return pl.ds(t, ROWS, stride=TILES)

    def pair_sums(part, target):
        squares = None
        for axis in range(3):
            mine = vel[axis, 1 + core * CHIPS + target, part_rows(part), :]
            other = partner_vel[axis, target, part_rows(part), :]
            sums[part, target, axis] = mine + other
            term = mine * mine + other * other
            squares = term if squares is None else squares + term
        sums[part, target, 3] = squares

    vel_up = remote(vel_ref.at[:, LAYERS - 1], vel.at[:, 0], vh_send.at[0], vh_recv.at[0], above)
    vel_down = remote(vel_ref.at[:, 0], vel.at[:, LAYERS + 1], vh_send.at[0], vh_recv.at[1], below)

    vel_up.start()
    vel_down.start()

    load_half(core).wait()
    for part in range(PARTS):
        pairs[part].wait_recv()
        for target in targets:
            pair_sums(part, target)
        pair_sums(part, chip)
        for place, target in enumerate(targets):
            remote(
                sums.at[part, target], arrived.at[part, chip], rs_send.at[0], rs_recv.at[part], peers[place]
            ).start()

    others = pl.ds(0, CHIPS - 1)
    own = core * CHIPS + chip
    for part in range(PARTS):
        remote(
            sums.at[part, others], arrived.at[part, others], rs_send.at[0], rs_recv.at[part], partner
        ).wait_recv()
        total = [
            (
                (sums[part, chip, i] + arrived[part, origins[0], i])
                + (arrived[part, origins[1], i] + arrived[part, origins[2], i])
            )
            + (
                (arrived[part, origins[3], i] + arrived[part, origins[4], i])
                + (arrived[part, origins[5], i] + arrived[part, origins[6], i])
            )
            for i in range(4)
        ]
        mean = [total[i] * (1.0 / 16) for i in range(3)]
        spread = total[3] * (1.0 / 16) - (mean[0] * mean[0] + mean[1] * mean[1] + mean[2] * mean[2])
        for i in range(3):
            flow[own, i, part_rows(part), :] = mean[i]
        flow[own, 3, part_rows(part), :] = BASE_VISCOSITY + EDDY_COEFF * TIME_STEP * spread
        piece = flow.at[own, :, part_rows(part)]
        for peer in peers:
            remote(piece, piece, ag_send.at[0], ag_recv.at[chip], peer).start()

    load_half(1 - core).wait()
    load_force.wait()
    vel_up.wait_recv()
    vel_down.wait_recv()

    def prepare(layer, carry):
        for axis in range(3):
            tiles = [vel[axis, layer + 1, tile_rows(t), :] for t in range(TILES)]
            for t in range(TILES):
                here = tiles[t]
                north = tiles[t + 1] if t + 1 < TILES else pltpu.roll(tiles[0], ROWS - 1, 0)
                south = tiles[t - 1] if t > 0 else pltpu.roll(tiles[TILES - 1], 1, 0)
                gaps = (
                    vel[axis, layer, tile_rows(t), :] - vel[axis, layer + 2, tile_rows(t), :],
                    south - north,
                    pltpu.roll(here, 1, 1) - pltpu.roll(here, LANES - 1, 1),
                )
                for i in range(3):
                    slopes[layer, axis, i, t] = (0.5 * TIME_STEP) * gaps[i]
                pre[layer, axis, t] = here + TIME_STEP * force[axis, layer, tile_rows(t), :]
        return carry

    lax.fori_loop(0, LAYERS, prepare, 0)

    def make_source(layer):
        for t in range(TILES):
            mean = [flow[layer, i, tile_rows(t), :] for i in range(3)]
            nu[HALO + layer, t] = flow[layer, 3, tile_rows(t), :]
            for axis in range(3):
                moved = mean[0] * slopes[layer, axis, 0, t] + mean[1] * slopes[layer, axis, 1, t]
                field_a[axis, HALO + layer, t] = pre[layer, axis, t] + (moved + mean[2] * slopes[layer, axis, 2, t])

    def chip_at(k):
        return shifted_chip(chip, k // 2, lax.rem(k, 2))

    def forward(at):
        layer = core * CHIPS + at
        return remote(flow.at[layer], flow.at[layer], fw_send.at[0], fw_recv.at[at], partner)

    forward(chip).start()

    def gather_step(k, carry):
        at = chip_at(k)
        layer = core * CHIPS + at
        remote(flow.at[layer], flow.at[layer], ag_send.at[0], ag_recv.at[at], partner).wait_recv()
        forward(at).start()
        return carry

    lax.fori_loop(1, CHIPS, gather_step, 0)

    def direct_sources(first):
        def body(i, carry):
            make_source(first + i)
            return carry

        lax.fori_loop(0, HALO, body, 0)

    def forwarded_sources(first):
        def body(i, carry):
            at = first + i - (1 - core) * CHIPS
            forward(at).wait_recv()
            make_source(first + i)
            return carry

        lax.fori_loop(0, HALO, body, 0)

    low, high = pl.ds(HALO, HALO), pl.ds(LAYERS, HALO)

    def side_of(side):
        device = (member, jnp.where(side == 1, above[1], below[1]))
        return (
            pl.ds(jnp.where(side == 1, LAYERS, HALO), HALO),
            pl.ds(jnp.where(side == 1, 0, HALO + LAYERS), HALO),
            device,
        )

    def nu_copy(side):
        inside, outside, device = side_of(side)
        return remote(nu.at[inside], nu.at[outside], nu_send.at[side], nu_recv.at[side], device)

    def source_copy(side, axis):
        inside, outside, device = side_of(side)
        return remote(
            field_a.at[axis, inside], field_a.at[axis, outside], src_send.at[0], src_recv.at[side, axis], device
        )

    def send_side(side):
        nu_copy(side).start()
        for axis in range(3):
            source_copy(side, axis).start()

    direct_sources(core * (LAYERS - HALO))
    send_side(core)
    forwarded_sources((1 - core) * (LAYERS - HALO))
    send_side(1 - core)
    direct_sources(HALO + core * HALO)
    forwarded_sources(HALO + (1 - core) * HALO)

    def make_weights(layer):
        centre = [nu[layer, t] for t in range(TILES)]
        for t in range(TILES):
            here = centre[t]
            north = centre[t + 1] if t + 1 < TILES else pltpu.roll(centre[0], ROWS - 1, 0)
            south = centre[t - 1] if t > 0 else pltpu.roll(centre[TILES - 1], 1, 0)
            around = (
                nu[layer + 1, t], nu[layer - 1, t], north, south,
                pltpu.roll(here, LANES - 1, 1), pltpu.roll(here, 1, 1),
            )
            faces = [here + other for other in around]
            total = ((faces[0] + faces[1]) + (faces[2] + faces[3])) + (faces[4] + faces[5])
            inverse = 1.0 / (1.0 + (0.5 * TIME_STEP) * total)
            scaled = (0.5 * TIME_STEP) * inverse
            for i in range(6):
                weights[layer, i, t] = faces[i] * scaled
            weights[layer, 6, t] = inverse

    def scale_source(layer, axis):
        for t in range(TILES):
            source[axis, layer, t] = field_a[axis, layer, t] * weights[layer, 6, t]

    def inner_weights(layer, carry):
        make_weights(layer)
        for axis in range(3):
            scale_source(layer, axis)
        return carry

    lax.fori_loop(HALO + 1, HALO + LAYERS - 1, inner_weights, 0)

    sizes = step_sizes(SWEEPS)

    def field_at(level):
        if level % HALO == 0:
            return field_a
        return (field_c, field_b)[level % 2]

    def sweep_tile(level, layer, axis, t, tiles, factors):
        old, new = field_at(level - 1), field_at(level)
        here = tiles[t]
        north = tiles[t + 1] if t + 1 < TILES else pltpu.roll(tiles[0], ROWS - 1, 0)
        south = tiles[t - 1] if t > 0 else pltpu.roll(tiles[TILES - 1], 1, 0)
        part_x = factors[0] * old[axis, layer + 1, t] + factors[1] * old[axis, layer - 1, t]
        part_y = factors[2] * north + factors[3] * south
        part_z = factors[4] * pltpu.roll(here, LANES - 1, 1) + factors[5] * pltpu.roll(here, 1, 1)
        change = ((source[axis, layer, t] - here) + part_x) + (part_y + part_z)
        value = here + sizes[level - 1] * change
        if level == SWEEPS:
            out_ref[axis, layer - HALO, pl.ds(t, ROWS, stride=TILES), :] = value
        else:
            new[axis, layer, t] = value

    def sweep_layer(level, layer, axes):
        old = field_at(level - 1)
        tiles = [[old[axis, layer, t] for t in range(TILES)] for axis in axes]
        for t in range(TILES):
            factors = [weights[layer, i, t] for i in range(6)]
            for axis, row in zip(axes, tiles):
                sweep_tile(level, layer, axis, t, row, factors)

    def sweep_inner(level, margin):
        count = LAYERS - 2 * margin

        def body(i, carry):
            for k in range(4):
                sweep_layer(level, HALO + margin + 4 * i + k, range(3))
            return carry

        lax.fori_loop(0, count // 4, body, 0)
        for k in range(count - count % 4, count):
            sweep_layer(level, HALO + margin + k, range(3))

    def sweep_outer(level, margin, axis):
        for layer in range(margin - HALO, margin):
            sweep_layer(level, HALO + layer, [axis])
            sweep_layer(level, HALO + LAYERS - 1 - layer, [axis])

    for level in range(1, HALO + 1):
        sweep_inner(level, level)
    remote(partner_vel, partner_vel, pair_send.at[0], pair_recv.at[0], partner).wait_send()
    remote(vel.at[:, pl.ds(0, 2)], vel.at[:, pl.ds(0, 2)], vh_send.at[0], vh_recv.at[0], above).wait_send()
    remote(sums.at[:, others], arrived.at[:, others], rs_send.at[0], rs_recv.at[0], partner).wait_send()
    remote(sums.at[:, others], arrived.at[:, others], ag_send.at[0], ag_recv.at[0], partner).wait_send()
    half = pl.ds(0, CHIPS)
    remote(flow.at[half], flow.at[half], fw_send.at[0], fw_recv.at[0], partner).wait_send()
    nu_copy(0).wait()
    nu_copy(1).wait()

    def outer_weights(layer, carry):
        make_weights(layer)
        make_weights(layer + LAYERS + HALO - 2)
        return carry

    lax.fori_loop(1, HALO + 1, outer_weights, 0)

    def field_copies(axis):
        return [
            remote(field_a.at[axis, low], halo_high.at[axis], mid_send.at[0], mid_recv.at[0, axis], below),
            remote(field_a.at[axis, high], halo_low.at[axis], mid_send.at[0], mid_recv.at[1, axis], above),
        ]

    def first_outer(axis, carry):
        for side in range(2):
            source_copy(side, axis).wait_recv()
        for layer in range(1, HALO + 1):
            scale_source(layer, axis)
            scale_source(layer + LAYERS + HALO - 2, axis)
        for level in range(1, HALO + 1):
            sweep_outer(level, level, axis)
        for copy in field_copies(axis):
            copy.start()
        return carry

    outer = pl.ds(0, 2 * HALO)
    remote(field_a.at[:, outer], field_a.at[:, outer], src_send.at[0], src_recv.at[0, 0], partner).wait_send()
    lax.fori_loop(0, 3, first_outer, 0)
    for level in range(1, HALO + 1):
        sweep_inner(HALO + level, level)

    def second_outer(axis, carry):
        for copy in field_copies(axis):
            copy.wait_recv()
        for layer in range(HALO):
            for t in range(TILES):
                field_a[axis, layer, t] = halo_low[axis, layer, t]
                field_a[axis, HALO + LAYERS + layer, t] = halo_high[axis, layer, t]
        for level in range(1, HALO + 1):
            sweep_outer(HALO + level, level, axis)
        return carry

    lax.fori_loop(0, 3, second_outer, 0)

    remote(field_a.at[:, outer], field_a.at[:, outer], mid_send.at[0], mid_recv.at[0, 0], partner).wait_send()


def per_device(velocity, forcing):
    f32 = jnp.float32
    full = LAYERS + 2 * HALO
    dma = pltpu.SemaphoreType.DMA
    tile = (ROWS, LANES)
    plane = (TILES * ROWS, LANES)
    result = pl.pallas_call(
        kernel,
        out_shape=jax.ShapeDtypeStruct(velocity.shape[1:], f32),
        in_specs=[pl.BlockSpec(memory_space=pltpu.MemorySpace.HBM)] * 2,
        out_specs=pl.BlockSpec(memory_space=pltpu.VMEM),
        scratch_shapes=[
            pltpu.VMEM((3, LAYERS + 2, *plane), f32),
            pltpu.VMEM((3, LAYERS, *plane), f32),
            pltpu.VMEM((3, CHIPS, *plane), f32),
            pltpu.VMEM((PARTS, CHIPS, 4, *tile), f32),
            pltpu.VMEM((PARTS, CHIPS, 4, *tile), f32),
            pltpu.VMEM((LAYERS, 4, *plane), f32),
            pltpu.VMEM((LAYERS, 3, TILES, *tile), f32),
            pltpu.VMEM((LAYERS, 3, 3, TILES, *tile), f32),
            pltpu.VMEM((full, TILES, *tile), f32),
            pltpu.VMEM((full, 7, TILES, *tile), f32),
            pltpu.VMEM((3, full, TILES, *tile), f32),
            pltpu.VMEM((3, full, TILES, *tile), f32),
            pltpu.VMEM((3, full, TILES, *tile), f32),
            pltpu.VMEM((3, full, TILES, *tile), f32),
            pltpu.VMEM((3, HALO, TILES, *tile), f32),
            pltpu.VMEM((3, HALO, TILES, *tile), f32),
            dma((3,)), dma((1,)), dma((PARTS,)),
            dma((1,)), dma((PARTS,)),
            dma((1,)), dma((CHIPS,)),
            dma((1,)), dma((CHIPS,)),
            dma((1,)), dma((2,)),
            dma((2,)), dma((2,)),
            dma((1,)), dma((2, 3)),
            dma((1,)), dma((2, 3)),
        ],
        compiler_params=pltpu.CompilerParams(
            collective_id=0, has_side_effects=True, vmem_limit_bytes=40 * 1024 * 1024
        ),
    )(
        pltpu.with_memory_space_constraint(velocity[0], pltpu.MemorySpace.HBM),
        pltpu.with_memory_space_constraint(forcing[0], pltpu.MemorySpace.HBM),
    )
    return result[None]


def solution(mesh):
    spec = P("member", None, "sub", None, None)
    return jax.shard_map(per_device, mesh=mesh, in_specs=(spec, spec), out_specs=spec, check_vma=False)
```

```python
import functools
import math

import jax
import jax.numpy as jnp
from jax import lax
from jax.experimental import pallas as pl
from jax.experimental.pallas import tpu as pltpu
from jax.sharding import PartitionSpec as P

MESH = pl.DeviceIdType.MESH
SWEEPS = 8
TIME_STEP = 0.25
EDDY_COEFF = 1.0
BASE_VISCOSITY = 1.0
LOWER_EDGE = 0.1
UPPER_EDGE = 1.9

LAYERS = 16
TILES = 4
ROWS = 8
LANES = 128
CHIPS = 8
HALO = 4
PARTS = 4
ORDER = ((2, 1), (1, 1), (3, 1), (2, 0), (1, 0), (3, 0), (0, 1))


def step_sizes(sweep_count):
    middle = (UPPER_EDGE + LOWER_EDGE) / 2
    radius = (UPPER_EDGE - LOWER_EDGE) / 2
    return [
        1.0 / (middle + radius * math.cos(math.pi * (2 * position + 1) / (2 * sweep_count)))
        for position in range(sweep_count)
    ]


def shifted_chip(chip, dx, dy):
    x, y = chip // 2, lax.rem(chip, 2)
    return lax.rem(x + dx, 4) * 2 + lax.rem(y + dy, 2)


def kernel(
    vel_ref, force_ref, out_ref,
    vel, force, partner_vel, sums, arrived, flow, pre, slopes, nu, weights, source, field_a, field_b, field_c, halo_low, halo_high,
    load_sem, pair_send, pair_recv, rs_send, rs_recv, ag_send, ag_recv, fw_send, fw_recv,
    vh_send, vh_recv, nu_send, nu_recv, src_send, src_recv, mid_send, mid_recv,
):
    member, sub = lax.axis_index("member"), lax.axis_index("sub")
    chip, core = member // 2, lax.rem(member, 2)
    subs = lax.axis_size("sub")
    above = (member, lax.rem(sub + 1, subs))
    below = (member, lax.rem(sub + subs - 1, subs))
    partner = (chip * 2 + 1 - core, sub)
    peers = [(shifted_chip(chip, dx, dy) * 2 + core, sub) for dx, dy in ORDER]
    targets = [shifted_chip(chip, dx, dy) for dx, dy in ORDER]
    origins = [shifted_chip(chip, 4 - dx, dy) for dx, dy in ORDER]

    def remote(src, dst, send, recv, device):
        return pltpu.make_async_remote_copy(
            src_ref=src, dst_ref=dst, send_sem=send, recv_sem=recv, device_id=device, device_id_type=MESH
        )

    def load_half(half):
        return pltpu.make_async_copy(
            vel_ref.at[:, pl.ds(half * CHIPS, CHIPS)], vel.at[:, pl.ds(1 + half * CHIPS, CHIPS)], load_sem.at[half]
        )

    load_force = pltpu.make_async_copy(force_ref, force, load_sem.at[2])
    load_half(core).start()
    load_half(1 - core).start()
    load_force.start()

    barrier = pltpu.get_barrier_semaphore()
    greeted = [*peers, partner, above, below]
    for device in greeted:
        pl.semaphore_signal(barrier, inc=1, device_id=device, device_id_type=MESH)
    pl.semaphore_wait(barrier, len(greeted))

    def part_rows(part):
        return pl.ds(part * ROWS, ROWS)

    pairs = [
        remote(
            vel_ref.at[:, pl.ds((1 - core) * CHIPS, CHIPS), part_rows(part)], partner_vel.at[:, :, part_rows(part)],
            pair_send.at[0], pair_recv.at[part], partner,
        )
        for part in range(PARTS)
    ]
    for copy in pairs:
        copy.start()

    def tile_rows(t):
        return pl.ds(t, ROWS, stride=TILES)

    def pair_sums(part, target):
        squares = None
        for axis in range(3):
            mine = vel[axis, 1 + core * CHIPS + target, part_rows(part), :]
            other = partner_vel[axis, target, part_rows(part), :]
            sums[part, target, axis] = mine + other
            term = mine * mine + other * other
            squares = term if squares is None else squares + term
        sums[part, target, 3] = squares

    vel_up = remote(vel_ref.at[:, LAYERS - 1], vel.at[:, 0], vh_send.at[0], vh_recv.at[0], above)
    vel_down = remote(vel_ref.at[:, 0], vel.at[:, LAYERS + 1], vh_send.at[0], vh_recv.at[1], below)

    vel_up.start()
    vel_down.start()

    load_half(core).wait()
    for part in range(PARTS):
        pairs[part].wait_recv()
        for target in targets:
            pair_sums(part, target)
        pair_sums(part, chip)
        for place, target in enumerate(targets):
            remote(
                sums.at[part, target], arrived.at[part, chip], rs_send.at[0], rs_recv.at[part], peers[place]
            ).start()

    others = pl.ds(0, CHIPS - 1)
    own = core * CHIPS + chip
    for part in range(PARTS):
        remote(
            sums.at[part, others], arrived.at[part, others], rs_send.at[0], rs_recv.at[part], partner
        ).wait_recv()
        total = [
            (
                (sums[part, chip, i] + arrived[part, origins[0], i])
                + (arrived[part, origins[1], i] + arrived[part, origins[2], i])
            )
            + (
                (arrived[part, origins[3], i] + arrived[part, origins[4], i])
                + (arrived[part, origins[5], i] + arrived[part, origins[6], i])
            )
            for i in range(4)
        ]
        mean = [total[i] * (1.0 / 16) for i in range(3)]
        spread = total[3] * (1.0 / 16) - (mean[0] * mean[0] + mean[1] * mean[1] + mean[2] * mean[2])
        for i in range(3):
            flow[own, i, part_rows(part), :] = mean[i]
        flow[own, 3, part_rows(part), :] = BASE_VISCOSITY + EDDY_COEFF * TIME_STEP * spread
        piece = flow.at[own, :, part_rows(part)]
        for peer in peers:
            remote(piece, piece, ag_send.at[0], ag_recv.at[chip], peer).start()

    load_half(1 - core).wait()
    load_force.wait()
    vel_up.wait_recv()
    vel_down.wait_recv()

    def prepare(layer, carry):
        for axis in range(3):
            tiles = [vel[axis, layer + 1, tile_rows(t), :] for t in range(TILES)]
            for t in range(TILES):
                here = tiles[t]
                north = tiles[t + 1] if t + 1 < TILES else pltpu.roll(tiles[0], ROWS - 1, 0)
                south = tiles[t - 1] if t > 0 else pltpu.roll(tiles[TILES - 1], 1, 0)
                gaps = (
                    vel[axis, layer, tile_rows(t), :] - vel[axis, layer + 2, tile_rows(t), :],
                    south - north,
                    pltpu.roll(here, 1, 1) - pltpu.roll(here, LANES - 1, 1),
                )
                for i in range(3):
                    slopes[layer, axis, i, t] = (0.5 * TIME_STEP) * gaps[i]
                pre[layer, axis, t] = here + TIME_STEP * force[axis, layer, tile_rows(t), :]
        return carry

    lax.fori_loop(0, LAYERS, prepare, 0)

    def make_source(layer):
        for t in range(TILES):
            mean = [flow[layer, i, tile_rows(t), :] for i in range(3)]
            nu[HALO + layer, t] = flow[layer, 3, tile_rows(t), :]
            for axis in range(3):
                moved = mean[0] * slopes[layer, axis, 0, t] + mean[1] * slopes[layer, axis, 1, t]
                field_a[axis, HALO + layer, t] = pre[layer, axis, t] + (moved + mean[2] * slopes[layer, axis, 2, t])

    def forward(at):
        layer = core * CHIPS + at
        return remote(flow.at[layer], flow.at[layer], fw_send.at[0], fw_recv.at[at], partner)

    forward(chip).start()

    def gather_step(k, carry):
        at = lax.rem(k + core * (CHIPS - HALO), CHIPS)
        layer = core * CHIPS + at

        @pl.when(at != chip)
        def _():
            remote(flow.at[layer], flow.at[layer], ag_send.at[0], ag_recv.at[at], partner).wait_recv()
            forward(at).start()

        return carry

    lax.fori_loop(0, CHIPS, gather_step, 0)

    def direct_sources(first):
        def body(i, carry):
            make_source(first + i)
            return carry

        lax.fori_loop(0, HALO, body, 0)

    def forwarded_sources(first):
        def body(i, carry):
            at = first + i - (1 - core) * CHIPS
            forward(at).wait_recv()
            make_source(first + i)
            return carry

        lax.fori_loop(0, HALO, body, 0)

    low, high = pl.ds(HALO, HALO), pl.ds(LAYERS, HALO)

    def side_of(side):
        device = (member, jnp.where(side == 1, above[1], below[1]))
        return (
            pl.ds(jnp.where(side == 1, LAYERS, HALO), HALO),
            pl.ds(jnp.where(side == 1, 0, HALO + LAYERS), HALO),
            device,
        )

    def nu_copy(side):
        inside, outside, device = side_of(side)
        return remote(nu.at[inside], nu.at[outside], nu_send.at[side], nu_recv.at[side], device)

    def source_copy(side, axis):
        inside, outside, device = side_of(side)
        return remote(
            field_a.at[axis, inside], field_a.at[axis, outside], src_send.at[0], src_recv.at[side, axis], device
        )

    def send_side(side):
        nu_copy(side).start()
        for axis in range(3):
            source_copy(side, axis).start()

    direct_sources(core * (LAYERS - HALO))
    send_side(core)
    forwarded_sources((1 - core) * (LAYERS - HALO))
    send_side(1 - core)
    direct_sources(HALO + core * HALO)
    forwarded_sources(HALO + (1 - core) * HALO)

    def make_weights(layer):
        centre = [nu[layer, t] for t in range(TILES)]
        for t in range(TILES):
            here = centre[t]
            north = centre[t + 1] if t + 1 < TILES else pltpu.roll(centre[0], ROWS - 1, 0)
            south = centre[t - 1] if t > 0 else pltpu.roll(centre[TILES - 1], 1, 0)
            around = (
                nu[layer + 1, t], nu[layer - 1, t], north, south,
                pltpu.roll(here, LANES - 1, 1), pltpu.roll(here, 1, 1),
            )
            faces = [here + other for other in around]
            total = ((faces[0] + faces[1]) + (faces[2] + faces[3])) + (faces[4] + faces[5])
            inverse = 1.0 / (1.0 + (0.5 * TIME_STEP) * total)
            scaled = (0.5 * TIME_STEP) * inverse
            for i in range(6):
                weights[layer, i, t] = faces[i] * scaled
            weights[layer, 6, t] = inverse

    def scale_source(layer, axis):
        for t in range(TILES):
            source[axis, layer, t] = field_a[axis, layer, t] * weights[layer, 6, t]

    def inner_weights(layer, carry):
        make_weights(layer)
        for axis in range(3):
            scale_source(layer, axis)
        return carry

    lax.fori_loop(HALO + 1, HALO + LAYERS - 1, inner_weights, 0)

    sizes = step_sizes(SWEEPS)

    def field_at(level):
        if level % HALO == 0:
            return field_a
        return (field_c, field_b)[level % 2]

    def sweep_tile(level, layer, axis, t, tiles, factors):
        old, new = field_at(level - 1), field_at(level)
        here = tiles[t]
        north = tiles[t + 1] if t + 1 < TILES else pltpu.roll(tiles[0], ROWS - 1, 0)
        south = tiles[t - 1] if t > 0 else pltpu.roll(tiles[TILES - 1], 1, 0)
        part_x = factors[0] * old[axis, layer + 1, t] + factors[1] * old[axis, layer - 1, t]
        part_y = factors[2] * north + factors[3] * south
        part_z = factors[4] * pltpu.roll(here, LANES - 1, 1) + factors[5] * pltpu.roll(here, 1, 1)
        change = ((source[axis, layer, t] - here) + part_x) + (part_y + part_z)
        value = here + sizes[level - 1] * change
        if level == SWEEPS:
            out_ref[axis, layer - HALO, pl.ds(t, ROWS, stride=TILES), :] = value
        else:
            new[axis, layer, t] = value

    def sweep_layer(level, layer, axes):
        old = field_at(level - 1)
        tiles = [[old[axis, layer, t] for t in range(TILES)] for axis in axes]
        for t in range(TILES):
            factors = [weights[layer, i, t] for i in range(6)]
            for axis, row in zip(axes, tiles):
                sweep_tile(level, layer, axis, t, row, factors)

    def sweep_inner(level, margin):
        count = LAYERS - 2 * margin

        def body(i, carry):
            for k in range(4):
                sweep_layer(level, HALO + margin + 4 * i + k, range(3))
            return carry

        lax.fori_loop(0, count // 4, body, 0)
        for k in range(count - count % 4, count):
            sweep_layer(level, HALO + margin + k, range(3))

    def sweep_outer(level, margin, axis):
        for layer in range(margin - HALO, margin):
            sweep_layer(level, HALO + layer, [axis])
            sweep_layer(level, HALO + LAYERS - 1 - layer, [axis])

    for level in range(1, HALO + 1):
        sweep_inner(level, level)
    remote(partner_vel, partner_vel, pair_send.at[0], pair_recv.at[0], partner).wait_send()
    remote(vel.at[:, pl.ds(0, 2)], vel.at[:, pl.ds(0, 2)], vh_send.at[0], vh_recv.at[0], above).wait_send()
    remote(sums.at[:, others], arrived.at[:, others], rs_send.at[0], rs_recv.at[0], partner).wait_send()
    remote(sums.at[:, others], arrived.at[:, others], ag_send.at[0], ag_recv.at[0], partner).wait_send()
    half = pl.ds(0, CHIPS)
    remote(flow.at[half], flow.at[half], fw_send.at[0], fw_recv.at[0], partner).wait_send()
    nu_copy(0).wait()
    nu_copy(1).wait()

    def outer_weights(layer, carry):
        make_weights(layer)
        make_weights(layer + LAYERS + HALO - 2)
        return carry

    lax.fori_loop(1, HALO + 1, outer_weights, 0)

    def field_copies(axis):
        return [
            remote(field_a.at[axis, low], halo_high.at[axis], mid_send.at[0], mid_recv.at[0, axis], below),
            remote(field_a.at[axis, high], halo_low.at[axis], mid_send.at[0], mid_recv.at[1, axis], above),
        ]

    def first_outer(axis, carry):
        for side in range(2):
            source_copy(side, axis).wait_recv()
        for layer in range(1, HALO + 1):
            scale_source(layer, axis)
            scale_source(layer + LAYERS + HALO - 2, axis)
        for level in range(1, HALO + 1):
            sweep_outer(level, level, axis)
        for copy in field_copies(axis):
            copy.start()
        return carry

    outer = pl.ds(0, 2 * HALO)
    remote(field_a.at[:, outer], field_a.at[:, outer], src_send.at[0], src_recv.at[0, 0], partner).wait_send()
    lax.fori_loop(0, 3, first_outer, 0)
    for level in range(1, HALO + 1):
        sweep_inner(HALO + level, level)

    def second_outer(axis, carry):
        for copy in field_copies(axis):
            copy.wait_recv()
        for layer in range(HALO):
            for t in range(TILES):
                field_a[axis, layer, t] = halo_low[axis, layer, t]
                field_a[axis, HALO + LAYERS + layer, t] = halo_high[axis, layer, t]
        for level in range(1, HALO + 1):
            sweep_outer(HALO + level, level, axis)
        return carry

    lax.fori_loop(0, 3, second_outer, 0)

    remote(field_a.at[:, outer], field_a.at[:, outer], mid_send.at[0], mid_recv.at[0, 0], partner).wait_send()


def per_device(velocity, forcing):
    f32 = jnp.float32
    full = LAYERS + 2 * HALO
    dma = pltpu.SemaphoreType.DMA
    tile = (ROWS, LANES)
    plane = (TILES * ROWS, LANES)
    result = pl.pallas_call(
        kernel,
        out_shape=jax.ShapeDtypeStruct(velocity.shape[1:], f32),
        in_specs=[pl.BlockSpec(memory_space=pltpu.MemorySpace.HBM)] * 2,
        out_specs=pl.BlockSpec(memory_space=pltpu.VMEM),
        scratch_shapes=[
            pltpu.VMEM((3, LAYERS + 2, *plane), f32),
            pltpu.VMEM((3, LAYERS, *plane), f32),
            pltpu.VMEM((3, CHIPS, *plane), f32),
            pltpu.VMEM((PARTS, CHIPS, 4, *tile), f32),
            pltpu.VMEM((PARTS, CHIPS, 4, *tile), f32),
            pltpu.VMEM((LAYERS, 4, *plane), f32),
            pltpu.VMEM((LAYERS, 3, TILES, *tile), f32),
            pltpu.VMEM((LAYERS, 3, 3, TILES, *tile), f32),
            pltpu.VMEM((full, TILES, *tile), f32),
            pltpu.VMEM((full, 7, TILES, *tile), f32),
            pltpu.VMEM((3, full, TILES, *tile), f32),
            pltpu.VMEM((3, full, TILES, *tile), f32),
            pltpu.VMEM((3, full, TILES, *tile), f32),
            pltpu.VMEM((3, full, TILES, *tile), f32),
            pltpu.VMEM((3, HALO, TILES, *tile), f32),
            pltpu.VMEM((3, HALO, TILES, *tile), f32),
            dma((3,)), dma((1,)), dma((PARTS,)),
            dma((1,)), dma((PARTS,)),
            dma((1,)), dma((CHIPS,)),
            dma((1,)), dma((CHIPS,)),
            dma((1,)), dma((2,)),
            dma((2,)), dma((2,)),
            dma((1,)), dma((2, 3)),
            dma((1,)), dma((2, 3)),
        ],
        compiler_params=pltpu.CompilerParams(
            collective_id=0, has_side_effects=True, vmem_limit_bytes=40 * 1024 * 1024
        ),
    )(
        pltpu.with_memory_space_constraint(velocity[0], pltpu.MemorySpace.HBM),
        pltpu.with_memory_space_constraint(forcing[0], pltpu.MemorySpace.HBM),
    )
    return result[None]


def solution(mesh):
    spec = P("member", None, "sub", None, None)
    return jax.shard_map(per_device, mesh=mesh, in_specs=(spec, spec), out_specs=spec, check_vma=False)
```
